32 devices in a mesh: groups: 2 (over x), context: 16 (over z, y, core).
Axes of the slice: x: 2, y: 2, z: 4, core: 2. Of those that a mesh axis runs over, the one named last changes fastest.
Arguments:
- q_store: bfloat16 [4096, 4096], P(('groups', 'context')), parts along dimension 0, may hold values from -6 to 6
- k_store: bfloat16 [4096, 4096], P(('groups', 'context')), parts along dimension 0, may hold values from -6 to 6
- v_store: bfloat16 [4096, 4096], P(('groups', 'context')), parts along dimension 0, may hold values from -6 to 6
- plan: int32 [32, 128], P(('groups', 'context')), parts along dimension 0, may hold values from 0 to 127, each once within a row
- doc_ids: int32 [4096], P(('groups', 'context')), parts along dimension 0, may hold values from 0 to 3, never falling along the last dimension, each value on 1 to 1024 neighbouring positions
- gain: float32 [4096], replicated, may hold values from 0.5 to 1.5
Outputs:
- out_store: bfloat16 [4096, 4096], P(('groups', 'context')), parts along dimension 0
The draws below stay inside these ranges and needn't reach their ends.
There are 2 independent parts, one for each index of `groups`. The reference program is written for one: setup_inputs(seed, part) draws one part's arguments, and reference() takes and returns one part's arrays. A program takes and returns all parts, laid end to end along the dimension named above; an argument that names none is the same for every part. Nothing has to cross between parts.
Inputs may be any that keep to these rules, and one draw needn't show every extreme that they name: Each row of plan names every offset below 128 once. `doc_ids`: never falls along positions; each document holds 1 to 1024 positions.
All inputs are finite; a program needn't handle non-finite values.
Results may differ from the reference program's by a relative error of at most 0.005.
Values may be sent and summed in bfloat16 or wider, within the bound.
No kernel may reach another device: no remote copies, remote signals or barrier semaphores. Data moves between devices by JAX's collectives and lax.ppermute only.
A program may use at most 320 MiB of HBM per device.

```python
import math
import jax
import jax.numpy as jnp
import numpy as np
from jax import lax

HEADS = 32
HEAD_DIM = 128
SPAN = 128
DOCS = 4
TOK_DEV = 128
TOKENS = 2048
N_CONTEXT = 16


def levels(stream_key, extent, cuts, least, largest):
    def one(dim, parts):
        heights = jax.random.uniform(jax.random.fold_in(jax.random.fold_in(stream_key, 6), dim), (parts,), jnp.float32, least / len(cuts), largest / len(cuts))
        return jnp.repeat(jnp.exp(heights), extent[dim] // parts).reshape((-1,) + (1,) * (len(extent) - dim - 1))

    loudness = one(*cuts[0])
    for cut in cuts[1:]:
        loudness = loudness * one(*cut)
    return loudness


def profile(number_of, total, limit, slope):
    weights = [(1 << 20) // math.isqrt(standing ** slope) + 1 for standing in range(2, number_of + 1)]
    spare, given = total - limit - (number_of - 1), [1] * (number_of - 1)
    while spare > 0:
        candidates = [i for i in range(number_of - 1) if given[i] < limit]
        mass, remaining = sum([weights[i] for i in candidates]), spare
        for i in candidates:
            more = min(limit - given[i], max(1, remaining * weights[i] // mass), spare)
            given[i] = given[i] + more
            spare = spare - more
    return np.array([limit] + given)


def ragged(stream_key, count, total, most, slope):
    if count == 2:
        one = jax.random.randint(stream_key, (), max(1, total - most), min(most, total - 1) + 1)
        return jnp.stack([one, total - one])
    sizes = jnp.asarray(profile(count, total, most, slope), jnp.int32)
    couples = (count - 1) // 2
    giver, receiver = sizes[1:1 + 2 * couples:2], sizes[2:2 + 2 * couples:2]
    margin = jnp.minimum(giver - 1, most - receiver)
    moved = jax.random.randint(jax.random.fold_in(stream_key, 1), (couples,), 0, 1 << 20) % (margin + 1)
    sizes = sizes.at[1:1 + 2 * couples:2].set(giver - moved).at[2:2 + 2 * couples:2].set(receiver + moved)
    return sizes[jax.random.permutation(jax.random.fold_in(stream_key, 2), count)]


def gaussian(stream_key, extent, scale, reach, split=(), kind=jnp.bfloat16):
    level = levels(stream_key, extent, split, -0.22, 0.18) if split else 1.0
    values = jax.random.normal(stream_key, extent, jnp.float32) * scale * level
    return jnp.minimum(jnp.maximum(values, -reach), reach).astype(kind)


def setup_inputs(seed: int = 0, part: int = 0) -> dict:
    keys = jax.random.split(jax.random.key(seed), 7)
    own_keys = jax.random.split(jax.random.fold_in(keys[6], part), 7)
    q_store = gaussian(own_keys[0], (TOKENS, HEADS * HEAD_DIM), 1.0, 6.0, ((0, 16),))
    k_store = gaussian(own_keys[1], (TOKENS, HEADS * HEAD_DIM), 1.0, 6.0, ((0, 16),))
    v_store = gaussian(own_keys[2], (TOKENS, HEADS * HEAD_DIM), 1.0, 6.0, ((0, 16),))
    plan = jax.vmap(lambda own: jax.random.permutation(own, TOK_DEV))(jax.random.split(own_keys[3], N_CONTEXT)).reshape((N_CONTEXT, TOK_DEV)).astype(jnp.int32)
    doc_ids = jnp.searchsorted(jnp.cumsum(ragged(own_keys[4], DOCS, TOKENS, TOKENS // 2, 1)), jnp.arange(TOKENS), side="right").astype(jnp.int32)
    gain = jnp.clip(1.0 + 0.1 * jax.random.normal(keys[5], (HEADS * HEAD_DIM,), jnp.float32), 0.5, 1.5)
    return {"q_store": q_store, "k_store": k_store, "v_store": v_store, "plan": plan, "doc_ids": doc_ids, "gain": gain}


def merge_states(earlier, later):
    early_state, early_doc = earlier
    late_state, late_doc = later
    keep_early = jnp.logical_or(early_doc == late_doc, late_doc < 0)
    merged = late_state + jnp.where(keep_early[:, None, None], early_state, jnp.zeros_like(early_state))
    return (merged, jnp.where(late_doc < 0, early_doc, late_doc))

def reference(q_store, k_store, v_store, plan, doc_ids, gain):
    devices = N_CONTEXT
    share = TOK_DEV // N_CONTEXT
    width = HEADS * HEAD_DIM
    row_index = jnp.arange(devices, dtype=jnp.int32)[:, None] * jnp.ones((1, TOK_DEV), jnp.int32)
    inverse = jnp.zeros((devices, TOK_DEV), jnp.int32).at[row_index, plan].set(jnp.ones((devices, 1), jnp.int32) * jnp.arange(TOK_DEV, dtype=jnp.int32)[None, :])

    def to_home(stored):
        arrived = stored.reshape(devices, devices, share, width).transpose(1, 0, 2, 3).reshape(devices, TOK_DEV, width)
        placed = jnp.take_along_axis(arrived, inverse[:, :, None], axis=1)
        return placed.reshape(TOKENS // SPAN, SPAN, HEADS, HEAD_DIM)
    queries = to_home(q_store)
    keys_home = to_home(k_store)
    values_home = to_home(v_store)
    docs = doc_ids.reshape(TOKENS // SPAN, SPAN)
    causal = jnp.arange(SPAN)[:, None] >= jnp.arange(SPAN)[None, :]

    def advance(carry, block):
        query_block, key_block, value_block, doc_block = block
        qf = query_block.astype(jnp.float32)
        kf = key_block.astype(jnp.float32)
        vf = value_block.astype(jnp.float32)
        scores = jnp.einsum('thd,shd->hts', qf, kf)
        allowed = jnp.logical_and(causal, doc_block[:, None] == doc_block[None, :])
        weights = jnp.where(allowed[None], scores, jnp.zeros_like(scores)).astype(jnp.bfloat16)
        weights = lax.optimization_barrier(weights).astype(jnp.float32)
        inner = jnp.einsum('hts,she->the', weights, vf)
        carry_state, carry_doc = carry
        rounded = lax.optimization_barrier(carry_state.astype(jnp.bfloat16)).astype(jnp.float32)
        match = (doc_block == carry_doc[0]).astype(jnp.float32)
        carried = jnp.einsum('thd,hde->the', qf, rounded) * match[:, None, None]
        tail = (doc_block == doc_block[-1]).astype(jnp.float32)
        block_state = jnp.einsum('shd,she->hde', kf * tail[:, None, None], vf)
        updated = merge_states(carry, (block_state, doc_block[-1:]))
        return (updated, inner + carried)
    start = (jnp.zeros((HEADS, HEAD_DIM, HEAD_DIM), jnp.float32), jnp.full((1,), -1, jnp.int32))
    final, mixed = lax.scan(advance, start, (queries, keys_home, values_home, docs))
    scale = lax.rsqrt(lax.optimization_barrier(jnp.mean(mixed * mixed, axis=-1, keepdims=True)) + 1e-06)
    normed = (mixed * scale * gain.reshape(HEADS, HEAD_DIM)).astype(jnp.bfloat16)
    normed = normed.reshape(devices, TOK_DEV, width)
    leaving = jnp.take_along_axis(normed, plan[:, :, None], axis=1)
    return leaving.reshape(devices, devices, share, width).transpose(1, 0, 2, 3).reshape(TOKENS, width)
```

```python
import functools

import jax
import jax.numpy as jnp
from jax import lax
from jax.experimental import pallas as pl
from jax.experimental.pallas import tpu as pltpu
from jax.sharding import PartitionSpec as P

HEAD_DIM = 128
SPAN = 128
AXIS = "context"


def entering(part, axis, combine, identity):
    place = lax.axis_index(axis)
    gathered = jax.tree.map(lambda a: lax.all_gather(a, axis), part)
    state = jax.tree.map(lambda a, e: jnp.zeros_like(a) + jnp.asarray(e, a.dtype), part, identity)

    def one(lap, state):
        return combine(
            state, jax.tree.map(lambda a: lax.dynamic_index_in_dim(a, lap, 0, False), gathered)
        )

    return lax.fori_loop(0, place, one, state)


def merge_states(earlier, later):
    early_state, early_doc = earlier
    late_state, late_doc = later
    keep_early = jnp.logical_or(early_doc == late_doc, late_doc < 0)
    merged = late_state + jnp.where(
        keep_early[:, None, None], early_state, jnp.zeros_like(early_state)
    )
    return (merged, jnp.where(late_doc < 0, early_doc, late_doc))


def at_home(q_store, k_store, v_store, plan, doc_ids, gain):
    token_count = q_store.shape[0]
    head_count = q_store.shape[1] // HEAD_DIM
    span_count = token_count // SPAN
    placed = plan.reshape(-1)
    inverse = (
        jnp.zeros((token_count,), jnp.int32)
        .at[placed]
        .set(jnp.arange(token_count, dtype=jnp.int32))
    )

    def settle(arrived):
        return jnp.take(arrived, inverse, axis=0).reshape(span_count, SPAN, head_count, HEAD_DIM)

    docs = doc_ids.reshape(span_count, SPAN)
    last_doc = docs[:, -1]
    query_rows, key_rows, value_rows = (
        lax.all_to_all(q_store, AXIS, split_axis=0, concat_axis=0, tiled=True),
        lax.all_to_all(k_store, AXIS, split_axis=0, concat_axis=0, tiled=True),
        lax.all_to_all(v_store, AXIS, split_axis=0, concat_axis=0, tiled=True),
    )
    keys_home = settle(key_rows)
    values_home = settle(value_rows)
    tail_mask = (docs == last_doc[:, None]).astype(jnp.bfloat16)
    span_states = jnp.einsum(
        "cshd,cshe->chde",
        keys_home * tail_mask[:, :, None, None],
        values_home,
        preferred_element_type=jnp.float32,
    )
    device_part = (span_states[0], last_doc)
    identity = (jnp.zeros_like(span_states[0]), jnp.full((1,), -1, jnp.int32))
    running = entering(device_part, AXIS, merge_states, identity)
    carry_states = running[0].astype(jnp.bfloat16)[None]
    queries = settle(query_rows)
    causal = jnp.arange(SPAN)[:, None] >= jnp.arange(SPAN)[None, :]
    allowed = jnp.logical_and(causal[None], docs[:, :, None] == docs[:, None, :])
    scores = jnp.einsum("cthd,cshd->chts", queries, keys_home, preferred_element_type=jnp.float32)
    weights = jnp.where(allowed[:, None], scores, 0.0).astype(jnp.bfloat16)
    inner = jnp.einsum("chts,cshe->cthe", weights, values_home, preferred_element_type=jnp.float32)
    match = (docs == running[1][:, None]).astype(jnp.bfloat16)
    carried = jnp.einsum(
        "cthd,chde->cthe",
        queries * match[:, :, None, None],
        carry_states,
        preferred_element_type=jnp.float32,
    )
    mixed = inner + carried
    scale = lax.rsqrt(jnp.mean(mixed * mixed, axis=-1, keepdims=True) + 1e-06)
    normed = (mixed * scale * gain.reshape(head_count, HEAD_DIM)).astype(jnp.bfloat16)
    normed = normed.reshape(token_count, head_count * HEAD_DIM)
    leaving = jnp.take(normed, placed, axis=0)
    return lax.all_to_all(leaving, AXIS, split_axis=0, concat_axis=0, tiled=True)


def pack_kernel(n, share, width, plan_ref, doc_ref, q_ref, k_ref, v_ref, *rest):
    pieces, sems = rest[:n], rest[n]
    me = lax.axis_index(AXIS)
    copies = []
    for m in range(n):
        to = pl.multiple_of(jnp.bitwise_xor(me, m) * width, width)
        for a, ref in enumerate((q_ref, k_ref, v_ref)):
            copy = pltpu.make_async_copy(
                ref.at[:, :, pl.ds(to, width)],
                pieces[m].at[pl.ds(a * n, n)],
                sems.at[m, a],
            )
            copy.start()
            copies.append(copy)
    offsets = plan_ref[...]
    hit = lax.broadcasted_iota(jnp.int32, (SPAN, SPAN), 0) == offsets
    docs = jnp.dot(
        jnp.broadcast_to(doc_ref[...].astype(jnp.bfloat16), (8, SPAN)),
        jnp.where(hit, 1.0, 0.0).astype(jnp.bfloat16),
        preferred_element_type=jnp.float32,
    )
    places = jnp.broadcast_to(offsets, (8, SPAN)).astype(jnp.float32)
    for m in range(n):
        pieces[m][3 * n, :, 0:SPAN] = places.astype(jnp.bfloat16)
        pieces[m][3 * n, :, SPAN : 2 * SPAN] = docs.astype(jnp.bfloat16)
    for copy in copies:
        copy.wait()


def pack(n, share, width, plan, docs, q, k, v):
    vmem, anywhere = pl.BlockSpec(memory_space=pltpu.VMEM), pl.BlockSpec(memory_space=pl.ANY)
    return pl.pallas_call(
        functools.partial(pack_kernel, n, share, width),
        out_shape=[jax.ShapeDtypeStruct((3 * n + 1, share, width), q.dtype)] * n,
        in_specs=[vmem, vmem, anywhere, anywhere, anywhere],
        out_specs=[vmem] * n,
        scratch_shapes=[pltpu.SemaphoreType.DMA((n, 3))],
        name="pack",
    )(plan, docs, q, k, v)


def attend_kernel(n, share, width, gain_ref, *rest):
    pieces, outs = rest[:n], rest[n : 2 * n]
    rows, places, docs, mixed_rows, state, sems, out_sems = rest[2 * n :]
    me = lax.axis_index(AXIS)
    heads = width // HEAD_DIM
    copies = []
    for m in range(n):
        peer = jnp.bitwise_xor(me, m)
        here = pl.ds(pl.multiple_of(peer * share, share), share)
        for a in range(3):
            copy = pltpu.make_async_copy(
                pieces[m].at[pl.ds(a * n, n)], rows.at[a, :, here, :], sems.at[m, a]
            )
            copy.start()
            copies.append(copy)
        copy = pltpu.make_async_copy(
            pieces[m].at[pl.ds(3 * n, 1), :, 0:SPAN], places.at[pl.ds(peer, 1)], sems.at[m, 3]
        )
        copy.start()
        copies.append(copy)
        copy = pltpu.make_async_copy(
            pieces[m].at[pl.ds(3 * n, 1), :, SPAN : 2 * SPAN],
            docs.at[pl.ds(peer, 1)],
            sems.at[m, 4],
        )
        copy.start()
        copies.append(copy)
    for copy in copies:
        copy.wait()
    state[...] = jnp.zeros_like(state)
    gains = [gain_ref[pl.ds(me * heads + h, 1), :] for h in range(heads)]

    def block(d, carry_doc):
        place_s = places[d].astype(jnp.float32)[0:1]
        doc_s = docs[d].astype(jnp.float32)[0:1]
        key_s = doc_s * SPAN + place_s
        key_t = jnp.transpose(jnp.broadcast_to(key_s, (SPAN, SPAN)))
        doc_t = jnp.floor(key_t * (1.0 / SPAN))
        allowed = jnp.logical_and(key_s <= key_t, key_s >= doc_t * SPAN)
        last_doc = jnp.broadcast_to(jnp.max(doc_s, axis=1, keepdims=True), (1, SPAN))
        match = doc_t == carry_doc
        tail = jnp.where(doc_s == last_doc, 1.0, 0.0).astype(jnp.bfloat16)
        kept = carry_doc == last_doc
        for h in range(heads):
            cols = slice(h * HEAD_DIM, (h + 1) * HEAD_DIM)
            q, k, v = rows[0, d, :, cols], rows[1, d, :, cols], rows[2, d, :, cols]
            turned = jnp.transpose(k)
            carry = state[h]
            scores = jnp.dot(q, turned, preferred_element_type=jnp.float32)
            carried = jnp.dot(q, carry.astype(jnp.bfloat16), preferred_element_type=jnp.float32)
            weights = jnp.where(allowed, scores, 0.0).astype(jnp.bfloat16)
            inner = jnp.dot(weights, v, preferred_element_type=jnp.float32)
            fresh = jnp.dot(turned * tail, v, preferred_element_type=jnp.float32)
            state[h] = fresh + jnp.where(kept, carry, 0.0)
            mixed = inner + jnp.where(match, carried, 0.0)
            scale = lax.rsqrt(jnp.mean(mixed * mixed, axis=-1, keepdims=True) + 1e-06)
            mixed_rows[d, :, cols] = (mixed * scale * gains[h]).astype(jnp.bfloat16)
        return last_doc

    lax.fori_loop(0, n, block, jnp.full((1, SPAN), -1.0, jnp.float32))
    copies = []
    for m in range(n):
        peer = jnp.bitwise_xor(me, m)
        here = pl.ds(pl.multiple_of(peer * share, share), share)
        copy = pltpu.make_async_copy(mixed_rows.at[:, here, :], outs[m], out_sems.at[m])
        copy.start()
        copies.append(copy)
    for copy in copies:
        copy.wait()


def attend(n, share, width, gain, pieces):
    vmem, anywhere = pl.BlockSpec(memory_space=pltpu.VMEM), pl.BlockSpec(memory_space=pl.ANY)
    dtype = pieces[0].dtype
    return pl.pallas_call(
        functools.partial(attend_kernel, n, share, width),
        out_shape=[jax.ShapeDtypeStruct((n, share, width), dtype)] * n,
        in_specs=[vmem] + [anywhere] * n,
        out_specs=[vmem] * n,
        scratch_shapes=[
            pltpu.VMEM((3, n, SPAN, width), dtype),
            pltpu.VMEM((n, share, SPAN), dtype),
            pltpu.VMEM((n, share, SPAN), dtype),
            pltpu.VMEM((n, SPAN, width), dtype),
            pltpu.VMEM((width // HEAD_DIM, HEAD_DIM, HEAD_DIM), jnp.float32),
            pltpu.SemaphoreType.DMA((n, 5)),
            pltpu.SemaphoreType.DMA((n,)),
        ],
        name="attend",
    )(gain, *pieces)


def unpack_kernel(n, share, width, *rest):
    pieces, out_ref, sems = rest[:n], rest[n], rest[n + 1]
    me = lax.axis_index(AXIS)
    copies = []
    for m in range(n):
        come = pl.multiple_of(jnp.bitwise_xor(me, m) * width, width)
        copy = pltpu.make_async_copy(
            pieces[m], out_ref.at[:, :, pl.ds(come, width)], sems.at[m]
        )
        copy.start()
        copies.append(copy)
    for copy in copies:
        copy.wait()


def unpack(n, share, width, pieces):
    vmem, anywhere = pl.BlockSpec(memory_space=pltpu.VMEM), pl.BlockSpec(memory_space=pl.ANY)
    return pl.pallas_call(
        functools.partial(unpack_kernel, n, share, width),
        out_shape=jax.ShapeDtypeStruct((n, share, n * width), pieces[0].dtype),
        in_specs=[vmem] * n,
        out_specs=anywhere,
        scratch_shapes=[pltpu.SemaphoreType.DMA((n,))],
        name="unpack",
    )(*pieces)


def exchange(n, pieces):
    far_first = sorted(range(1, n), key=lambda m: -(m // 2))
    sent = {
        m: lax.ppermute(pieces[m], AXIS, [(i, i ^ m) for i in range(n)]) for m in far_first
    }
    return [pieces[0]] + [sent[m] for m in range(1, n)]


def heads_apart(n, q_store, k_store, v_store, plan, doc_ids, gain):
    share = SPAN // n
    full = q_store.shape[1]
    width = full // n
    q, k, v = (a.reshape(n, share, full) for a in (q_store, k_store, v_store))
    pieces = pack(n, share, width, plan.reshape(1, SPAN), doc_ids.reshape(1, SPAN), q, k, v)
    pieces = exchange(n, pieces)
    pieces = attend(n, share, width, gain.reshape(full // HEAD_DIM, HEAD_DIM), pieces)
    pieces = exchange(n, pieces)
    return unpack(n, share, width, pieces).reshape(SPAN, full)


def solution(mesh):
    n = mesh.shape[AXIS]

    def on_device(q_store, k_store, v_store, plan, doc_ids, gain):
        heads = q_store.shape[1] // HEAD_DIM
        paired = n & (n - 1) == 0
        tiled = q_store.shape[0] == SPAN and SPAN % n == 0 and (SPAN // n) % 8 == 0
        if paired and tiled and heads % n == 0 and heads // n >= 2:
            return heads_apart(n, q_store, k_store, v_store, plan, doc_ids, gain)
        return at_home(q_store, k_store, v_store, plan, doc_ids, gain)

    return jax.shard_map(
        on_device,
        mesh=mesh,
        in_specs=(
            P(("groups", "context"), None),
            P(("groups", "context"), None),
            P(("groups", "context"), None),
            P(("groups", "context"), None),
            P(("groups", "context")),
            P(),
        ),
        out_specs=P(("groups", "context"), None),
        check_vma=False,
    )
```

```python
import functools

import jax
import jax.numpy as jnp
from jax import lax
from jax.experimental import pallas as pl
from jax.experimental.pallas import tpu as pltpu
from jax.sharding import PartitionSpec as P


HEAD_DIM = 128
SPAN = 128
AXIS = "context"


def entering(part, axis, combine, identity):
    place = lax.axis_index(axis)
    gathered = jax.tree.map(lambda a: lax.all_gather(a, axis), part)
    state = jax.tree.map(lambda a, e: jnp.zeros_like(a) + jnp.asarray(e, a.dtype), part, identity)

    def one(lap, state):
        return combine(
            state, jax.tree.map(lambda a: lax.dynamic_index_in_dim(a, lap, 0, False), gathered)
        )

    return lax.fori_loop(0, place, one, state)


def merge_states(earlier, later):
    early_state, early_doc = earlier
    late_state, late_doc = later
    keep_early = jnp.logical_or(early_doc == late_doc, late_doc < 0)
    merged = late_state + jnp.where(
        keep_early[:, None, None], early_state, jnp.zeros_like(early_state)
    )
    return (merged, jnp.where(late_doc < 0, early_doc, late_doc))


def at_home(q_store, k_store, v_store, plan, doc_ids, gain):
    token_count = q_store.shape[0]
    head_count = q_store.shape[1] // HEAD_DIM
    span_count = token_count // SPAN
    placed = plan.reshape(-1)
    inverse = (
        jnp.zeros((token_count,), jnp.int32)
        .at[placed]
        .set(jnp.arange(token_count, dtype=jnp.int32))
    )

    def settle(arrived):
        return jnp.take(arrived, inverse, axis=0).reshape(span_count, SPAN, head_count, HEAD_DIM)

    docs = doc_ids.reshape(span_count, SPAN)
    last_doc = docs[:, -1]
    query_rows, key_rows, value_rows = (
        lax.all_to_all(q_store, AXIS, split_axis=0, concat_axis=0, tiled=True),
        lax.all_to_all(k_store, AXIS, split_axis=0, concat_axis=0, tiled=True),
        lax.all_to_all(v_store, AXIS, split_axis=0, concat_axis=0, tiled=True),
    )
    keys_home = settle(key_rows)
    values_home = settle(value_rows)
    tail_mask = (docs == last_doc[:, None]).astype(jnp.bfloat16)
    span_states = jnp.einsum(
        "cshd,cshe->chde",
        keys_home * tail_mask[:, :, None, None],
        values_home,
        preferred_element_type=jnp.float32,
    )
    device_part = (span_states[0], last_doc)
    identity = (jnp.zeros_like(span_states[0]), jnp.full((1,), -1, jnp.int32))
    running = entering(device_part, AXIS, merge_states, identity)
    carry_states = running[0].astype(jnp.bfloat16)[None]
    queries = settle(query_rows)
    causal = jnp.arange(SPAN)[:, None] >= jnp.arange(SPAN)[None, :]
    allowed = jnp.logical_and(causal[None], docs[:, :, None] == docs[:, None, :])
    scores = jnp.einsum("cthd,cshd->chts", queries, keys_home, preferred_element_type=jnp.float32)
    weights = jnp.where(allowed[:, None], scores, 0.0).astype(jnp.bfloat16)
    inner = jnp.einsum("chts,cshe->cthe", weights, values_home, preferred_element_type=jnp.float32)
    match = (docs == running[1][:, None]).astype(jnp.bfloat16)
    carried = jnp.einsum(
        "cthd,chde->cthe",
        queries * match[:, :, None, None],
        carry_states,
        preferred_element_type=jnp.float32,
    )
    mixed = inner + carried
    scale = lax.rsqrt(jnp.mean(mixed * mixed, axis=-1, keepdims=True) + 1e-06)
    normed = (mixed * scale * gain.reshape(head_count, HEAD_DIM)).astype(jnp.bfloat16)
    normed = normed.reshape(token_count, head_count * HEAD_DIM)
    leaving = jnp.take(normed, placed, axis=0)
    return lax.all_to_all(leaving, AXIS, split_axis=0, concat_axis=0, tiled=True)


VMEM = pl.BlockSpec(memory_space=pltpu.VMEM)
ANY = pl.BlockSpec(memory_space=pl.ANY)
HBM = pl.BlockSpec(memory_space=pltpu.HBM)
ROOM = pltpu.CompilerParams(vmem_limit_bytes=24 << 20)
CHUNKS = (10, 6)


def slots(pairs):
    far = list(range(pairs - 1, pairs // 2 - 1, -1))
    near = [1, *range(pairs // 2 - 1, 1, -1)]
    return list(zip(far + near, near + far)) + [(0, 0)]


def place():
    me = lax.axis_index(AXIS)
    mine, side = lax.shift_right_logical(me, 1), jnp.bitwise_and(me, 1)
    return mine, side


def peers(pairs):
    mine, side = place()
    return [
        jnp.bitwise_xor(mine, jnp.where(side == 0, zero, one)) for zero, one in slots(pairs)
    ]


def start_all(copies):
    for copy in copies:
        copy.start()
    return copies


def wait_all(copies):
    for copy in copies:
        copy.wait()


def rows_of(pair, share):
    return pl.ds(pl.multiple_of(pair * share, share), share)


def pack_kernel(pairs, heads, first, count, plan_ref, doc_ref, q_ref, k_ref, v_ref, *rest):
    pieces = rest[:pairs]
    plans, docs, notes, sems, note_sems = rest[pairs:]
    share = SPAN // (2 * pairs)
    copies = []
    if first == 0:
        read = start_all(
            [
                pltpu.make_async_copy(plan_ref, plans, note_sems.at[pairs]),
                pltpu.make_async_copy(doc_ref, docs, note_sems.at[pairs + 1]),
            ]
        )
    tiles = count * heads
    for m, peer in enumerate(peers(pairs)):
        for a, ref in enumerate((q_ref, k_ref, v_ref)):
            room = pieces[m].at[pl.ds(a * tiles, tiles)]
            copy = pltpu.make_async_copy(
                ref.at[pl.ds(first, count), pl.ds(peer * heads, heads)],
                room.reshape(count, heads, share, HEAD_DIM),
                sems.at[m, a],
            )
            copies += start_all([copy])
    if first == 0:
        wait_all(read)
        lane = lax.broadcasted_iota(jnp.int32, (SPAN, SPAN), 1)
        other = lax.broadcasted_iota(jnp.int32, (SPAN, SPAN), 0)
        half, within = lane // (pairs * share), lane % (pairs * share)
        source = (within // share * 2 + half) * share + within % share
        order = jnp.where(other == source, 1.0, 0.0).astype(jnp.bfloat16)
        places = jnp.dot(
            jnp.broadcast_to(plans[...].astype(jnp.bfloat16), (share, SPAN)),
            order,
            preferred_element_type=jnp.float32,
        )
        hit = other.astype(jnp.float32) == places[0:1]
        docs_here = jnp.dot(
            jnp.broadcast_to(docs[...].astype(jnp.bfloat16), (share, SPAN)),
            jnp.where(hit, 1.0, 0.0).astype(jnp.bfloat16),
            preferred_element_type=jnp.float32,
        )
        row = lax.broadcasted_iota(jnp.int32, (share, SPAN), 0)
        notes[0] = jnp.where(row == 0, places, docs_here).astype(jnp.bfloat16)
        copies += start_all(
            [
                pltpu.make_async_copy(notes, pieces[m].at[pl.ds(3 * tiles, 1)], note_sems.at[m])
                for m in range(pairs)
            ]
        )
    wait_all(copies)


def pack(pairs, first, count, plan, docs, q, k, v):
    heads, share = q.shape[1] // pairs, q.shape[2]
    tiles = 3 * count * heads + (first == 0)
    shape = jax.ShapeDtypeStruct((tiles, share, HEAD_DIM), q.dtype)
    return pl.pallas_call(
        functools.partial(pack_kernel, pairs, heads, first, count),
        out_shape=[shape] * pairs,
        in_specs=[HBM] * 5,
        out_specs=[ANY] * pairs,
        scratch_shapes=[
            pltpu.VMEM((1, SPAN), jnp.int32),
            pltpu.VMEM((1, SPAN), jnp.int32),
            pltpu.VMEM((1, share, SPAN), q.dtype),
            pltpu.SemaphoreType.DMA((pairs, 3)),
            pltpu.SemaphoreType.DMA((pairs + 2,)),
        ],
        compiler_params=ROOM,
        name="pack",
    )(plan, docs, q, k, v)


def mark_kernel(x_ref, out_ref):
    pass


def mark(x):
    return pl.pallas_call(
        mark_kernel,
        out_shape=jax.ShapeDtypeStruct((8, SPAN), jnp.float32),
        in_specs=[ANY],
        out_specs=ANY,
        compiler_params=ROOM,
        name="mark",
    )(x)


def collect_kernel(pairs, share, start, marked, *rest):
    rest = rest[marked:]
    pieces = rest[:pairs]
    out_ref, sems = rest[pairs:]
    copies = [
        pltpu.make_async_copy(
            pieces[m].at[pl.ds(start, out_ref.shape[0])],
            out_ref.at[:, rows_of(peer, share), :],
            sems.at[m],
        )
        for m, peer in enumerate(peers(pairs))
    ]
    wait_all(start_all(copies))


def collect(pairs, start, stop, pieces, marked):
    _, share, width = pieces[0].shape
    return pl.pallas_call(
        functools.partial(collect_kernel, pairs, share, start, len(marked)),
        out_shape=jax.ShapeDtypeStruct((stop - start, pairs * share, width), pieces[0].dtype),
        in_specs=[ANY] * (pairs + len(marked)),
        out_specs=ANY,
        scratch_shapes=[pltpu.SemaphoreType.DMA((pairs,))],
        compiler_params=ROOM,
        name="collect",
    )(*marked, *pieces)


def attend_kernel(pairs, share, width, first, count, last, gain_ref, *rest):
    rest = list(rest)
    take = lambda k: [rest.pop(0) for _ in range(k)]
    given = take(3) if first else None
    queries, own, other = take(3)
    outs = take(pairs)
    kept = [] if last else take(3)
    state, mixed_rows, sems = rest
    half = pairs * share
    mine, side = place()
    heads = width // HEAD_DIM
    tiles = count * heads
    lower = side == 0
    if first:
        carry_doc = given[0][...]
        state[...] = given[1][...]
        lower_notes, upper_notes = given[2][:half], given[2][half:]
    else:
        carry_doc = jnp.full((1, SPAN), -1.0, jnp.float32)
        state[...] = jnp.zeros_like(state)
        lower_notes = jnp.where(lower, own[2 * tiles], other[2 * tiles])
        upper_notes = jnp.where(lower, other[2 * tiles], own[2 * tiles])
    if not last:
        kept[2][:half] = lower_notes
        kept[2][half:] = upper_notes
    gains = [gain_ref[pl.ds(mine * heads + h, 1), :] for h in range(heads)]

    def block(d, carry_doc):
        at = (first + d) // 2 * share
        said = (upper_notes if (first + d) % 2 else lower_notes)[at : at + share]
        said = said.astype(jnp.float32)
        said = jnp.where(lower, said, pltpu.roll(said, SPAN // 2, axis=1))
        place_s, doc_s = said[0:1], said[1:2]
        key_s = doc_s * SPAN + place_s
        key_t = jnp.transpose(jnp.broadcast_to(key_s, (SPAN, SPAN)))[:half]
        doc_t = jnp.floor(key_t * (1.0 / SPAN))
        allowed = jnp.logical_and(key_s <= key_t, key_s >= doc_t * SPAN)
        last_doc = jnp.broadcast_to(jnp.max(doc_s, axis=1, keepdims=True), (1, SPAN))
        match = doc_t == carry_doc
        tail = jnp.where(doc_s == last_doc, 1.0, 0.0).astype(jnp.bfloat16)
        keep = carry_doc == last_doc
        for h in range(heads):
            cols = slice(h * HEAD_DIM, (h + 1) * HEAD_DIM)
            tile = d * heads + h
            q = queries[tile]
            k, v = (
                jnp.concatenate([own[a * tiles + tile], other[a * tiles + tile]])
                for a in range(2)
            )
            turned = jnp.transpose(k)
            carry = state[h]
            scores = jnp.dot(q, turned, preferred_element_type=jnp.float32)
            carried = jnp.dot(q, carry.astype(jnp.bfloat16), preferred_element_type=jnp.float32)
            weights = jnp.where(allowed, scores, 0.0).astype(jnp.bfloat16)
            inner = jnp.dot(weights, v, preferred_element_type=jnp.float32)
            fresh = jnp.dot(turned * tail, v, preferred_element_type=jnp.float32)
            state[h] = fresh + jnp.where(keep, carry, 0.0)
            mixed = inner + jnp.where(match, carried, 0.0)
            scale = lax.rsqrt(jnp.mean(mixed * mixed, axis=-1, keepdims=True) + 1e-06)
            mixed_rows[d, :, cols] = (mixed * scale * gains[h]).astype(jnp.bfloat16)
        return last_doc

    copies = []
    for d in range(count):
        carry_doc = block(d, carry_doc)
        if d + 1 in (count // 2, count):
            done = pl.ds(0, count // 2) if d + 1 < count else pl.ds(count // 2, count - count // 2)
            copies += start_all(
                [
                    pltpu.make_async_copy(
                        mixed_rows.at[done, rows_of(peer, share), :],
                        outs[m].at[done],
                        sems.at[int(d + 1 == count), m],
                    )
                    for m, peer in enumerate(peers(pairs))
                ]
            )
    if not last:
        kept[0][...] = carry_doc
        kept[1][...] = state[...]
    wait_all(copies)


def attend(pairs, share, width, first, count, last, gain, queries, own, other, given):
    half, dtype = pairs * share, own.dtype
    state = (width // HEAD_DIM, HEAD_DIM, HEAD_DIM)
    kept = [
        jax.ShapeDtypeStruct((1, SPAN), jnp.float32),
        jax.ShapeDtypeStruct(state, jnp.float32),
        jax.ShapeDtypeStruct((2 * half, SPAN), dtype),
    ]
    kept, given = [] if last else kept, list(given) if first else []
    near = [
        pltpu.with_memory_space_constraint(x, pltpu.VMEM)
        for x in given + [queries, own, other]
    ]
    results = pl.pallas_call(
        functools.partial(attend_kernel, pairs, share, width, first, count, last),
        out_shape=[jax.ShapeDtypeStruct((count, share, width), dtype)] * pairs + kept,
        in_specs=[VMEM] * (4 + len(given)),
        out_specs=[ANY] * pairs + [VMEM] * len(kept),
        scratch_shapes=[
            pltpu.VMEM(state, jnp.float32),
            pltpu.VMEM((count, half, width), dtype),
            pltpu.SemaphoreType.DMA((2, pairs)),
        ],
        compiler_params=ROOM,
        name="attend",
    )(gain, *near)
    return results[:pairs], results[pairs:]


def unpack_kernel(pairs, width, spans, *rest):
    out_ref, sems = rest[-2:]
    copies = []
    for c, (first, count) in enumerate(spans):
        for m, peer in enumerate(peers(pairs)):
            come = pl.ds(pl.multiple_of(peer * width, width), width)
            copies.append(
                pltpu.make_async_copy(
                    rest[c * pairs + m], out_ref.at[pl.ds(first, count), :, come], sems.at[c, m]
                )
            )
    wait_all(start_all(copies))


def unpack(n, width, spans, pieces):
    share, dtype = pieces[0].shape[1], pieces[0].dtype
    pairs = n // 2
    return pl.pallas_call(
        functools.partial(unpack_kernel, pairs, width, spans),
        out_shape=jax.ShapeDtypeStruct((n, share, pairs * width), dtype),
        in_specs=[ANY] * (pairs * len(spans)),
        out_specs=ANY,
        scratch_shapes=[pltpu.SemaphoreType.DMA((len(spans), pairs))],
        compiler_params=ROOM,
        name="unpack",
    )(*pieces)


def swap(x, n, zero, one):
    return lax.ppermute(x, AXIS, [(i, i ^ (one if i & 1 else zero)) for i in range(n)])


def exchange(n, pieces):
    arrived = []
    for (zero, one), x in zip(slots(n // 2), pieces):
        arrived.append(swap(x, n, 2 * zero, 2 * one) if zero else x)
    return arrived


def heads_apart(n, q_store, k_store, v_store, plan, doc_ids, gain):
    share, pairs, full = SPAN // n, n // 2, q_store.shape[1]
    width = full // pairs
    stays = lambda a, *shape: pltpu.with_memory_space_constraint(a.reshape(shape), pltpu.HBM)
    heads = full // HEAD_DIM
    tiled = lambda a: a.reshape(n, share, heads, HEAD_DIM).transpose(0, 2, 1, 3)
    q, k, v = (stays(tiled(a), n, heads, share, HEAD_DIM) for a in (q_store, k_store, v_store))
    plan, docs = stays(plan, 1, SPAN), stays(doc_ids, 1, SPAN)
    gain = gain.reshape(heads, HEAD_DIM)
    parts = [c * n // sum(CHUNKS) for c in CHUNKS]
    spans = [(sum(parts[:c]), count) for c, count in enumerate(parts)]
    arrived = []
    for first, count in spans:
        pieces = pack(pairs, first, count, plan, docs, q, k, v)
        arrived.append(exchange(n, pieces))
    back, given, marked = [], None, []
    for (first, count), pieces in zip(spans, arrived):
        last = first + count == n
        marks = marked
        if not last:
            marks = marks + [mark(plan)]
        tiles = count * heads // pairs
        own = collect(pairs, tiles, pieces[0].shape[0], pieces, marks)
        other = swap(own, n, 1, 1)
        queries = collect(pairs, 0, tiles, pieces, [])
        pieces, given = attend(
            pairs, share, width, first, count, last, gain, queries, own, other, given
        )
        if not last:
            marked = [mark(pieces[-1])]
        back += exchange(n, pieces)
    return unpack(n, width, spans, back).reshape(SPAN, full)


def solution(mesh):
    n = mesh.shape[AXIS]

    def on_device(q_store, k_store, v_store, plan, doc_ids, gain):
        heads = q_store.shape[1] // HEAD_DIM
        paired = n & (n - 1) == 0
        tiled = q_store.shape[0] == SPAN and SPAN % n == 0 and (SPAN // n) % 8 == 0
        if paired and tiled and n >= 8 and heads % n == 0:
            return heads_apart(n, q_store, k_store, v_store, plan, doc_ids, gain)
        return at_home(q_store, k_store, v_store, plan, doc_ids, gain)

    return jax.shard_map(
        on_device,
        mesh=mesh,
        in_specs=(
            P(("groups", "context"), None),
            P(("groups", "context"), None),
            P(("groups", "context"), None),
            P(("groups", "context"), None),
            P(("groups", "context")),
            P(),
        ),
        out_specs=P(("groups", "context"), None),
        check_vma=False,
    )
```

```python
import functools

import jax
import jax.numpy as jnp
from jax import lax
from jax.experimental import pallas as pl
from jax.experimental.pallas import tpu as pltpu
from jax.sharding import PartitionSpec as P


HEAD_DIM = 128
SPAN = 128
AXIS = "context"


def entering(part, axis, combine, identity):
    place = lax.axis_index(axis)
    gathered = jax.tree.map(lambda a: lax.all_gather(a, axis), part)
    state = jax.tree.map(lambda a, e: jnp.zeros_like(a) + jnp.asarray(e, a.dtype), part, identity)

    def one(lap, state):
        return combine(
            state, jax.tree.map(lambda a: lax.dynamic_index_in_dim(a, lap, 0, False), gathered)
        )

    return lax.fori_loop(0, place, one, state)


def merge_states(earlier, later):
    early_state, early_doc = earlier
    late_state, late_doc = later
    keep_early = jnp.logical_or(early_doc == late_doc, late_doc < 0)
    merged = late_state + jnp.where(
        keep_early[:, None, None], early_state, jnp.zeros_like(early_state)
    )
    return (merged, jnp.where(late_doc < 0, early_doc, late_doc))


def at_home(q_store, k_store, v_store, plan, doc_ids, gain):
    token_count = q_store.shape[0]
    head_count = q_store.shape[1] // HEAD_DIM
    span_count = token_count // SPAN
    placed = plan.reshape(-1)
    inverse = (
        jnp.zeros((token_count,), jnp.int32)
        .at[placed]
        .set(jnp.arange(token_count, dtype=jnp.int32))
    )

    def settle(arrived):
        return jnp.take(arrived, inverse, axis=0).reshape(span_count, SPAN, head_count, HEAD_DIM)

    docs = doc_ids.reshape(span_count, SPAN)
    last_doc = docs[:, -1]
    query_rows, key_rows, value_rows = (
        lax.all_to_all(q_store, AXIS, split_axis=0, concat_axis=0, tiled=True),
        lax.all_to_all(k_store, AXIS, split_axis=0, concat_axis=0, tiled=True),
        lax.all_to_all(v_store, AXIS, split_axis=0, concat_axis=0, tiled=True),
    )
    keys_home = settle(key_rows)
    values_home = settle(value_rows)
    tail_mask = (docs == last_doc[:, None]).astype(jnp.bfloat16)
    span_states = jnp.einsum(
        "cshd,cshe->chde",
        keys_home * tail_mask[:, :, None, None],
        values_home,
        preferred_element_type=jnp.float32,
    )
    device_part = (span_states[0], last_doc)
    identity = (jnp.zeros_like(span_states[0]), jnp.full((1,), -1, jnp.int32))
    running = entering(device_part, AXIS, merge_states, identity)
    carry_states = running[0].astype(jnp.bfloat16)[None]
    queries = settle(query_rows)
    causal = jnp.arange(SPAN)[:, None] >= jnp.arange(SPAN)[None, :]
    allowed = jnp.logical_and(causal[None], docs[:, :, None] == docs[:, None, :])
    scores = jnp.einsum("cthd,cshd->chts", queries, keys_home, preferred_element_type=jnp.float32)
    weights = jnp.where(allowed[:, None], scores, 0.0).astype(jnp.bfloat16)
    inner = jnp.einsum("chts,cshe->cthe", weights, values_home, preferred_element_type=jnp.float32)
    match = (docs == running[1][:, None]).astype(jnp.bfloat16)
    carried = jnp.einsum(
        "cthd,chde->cthe",
        queries * match[:, :, None, None],
        carry_states,
        preferred_element_type=jnp.float32,
    )
    mixed = inner + carried
    scale = lax.rsqrt(jnp.mean(mixed * mixed, axis=-1, keepdims=True) + 1e-06)
    normed = (mixed * scale * gain.reshape(head_count, HEAD_DIM)).astype(jnp.bfloat16)
    normed = normed.reshape(token_count, head_count * HEAD_DIM)
    leaving = jnp.take(normed, placed, axis=0)
    return lax.all_to_all(leaving, AXIS, split_axis=0, concat_axis=0, tiled=True)


VMEM = pl.BlockSpec(memory_space=pltpu.VMEM)
ANY = pl.BlockSpec(memory_space=pl.ANY)
HBM = pl.BlockSpec(memory_space=pltpu.HBM)
ROOM = pltpu.CompilerParams(vmem_limit_bytes=24 << 20)
CHUNKS = (10, 6)


def slots(pairs):
    far = list(range(pairs - 1, pairs // 2 - 1, -1))
    near = [1, *range(pairs // 2 - 1, 1, -1)]
    return list(zip(far + near, near + far)) + [(0, 0)]


def place():
    me = lax.axis_index(AXIS)
    mine, side = lax.shift_right_logical(me, 1), jnp.bitwise_and(me, 1)
    return mine, side


def peers(pairs):
    mine, side = place()
    return [
        jnp.bitwise_xor(mine, jnp.where(side == 0, zero, one)) for zero, one in slots(pairs)
    ]


def start_all(copies):
    for copy in copies:
        copy.start()
    return copies


def wait_all(copies):
    for copy in copies:
        copy.wait()


def rows_of(pair, share):
    return pl.ds(pl.multiple_of(pair * share, share), share)


def pack_kernel(pairs, heads, first, count, chosen, plan_ref, doc_ref, q_ref, k_ref, v_ref, *rest):
    pieces = dict(zip(chosen, rest))
    plans, docs, notes, sems, note_sems = rest[len(chosen) :]
    share = SPAN // (2 * pairs)
    copies = []
    if first == 0:
        read = start_all(
            [
                pltpu.make_async_copy(plan_ref, plans, note_sems.at[pairs]),
                pltpu.make_async_copy(doc_ref, docs, note_sems.at[pairs + 1]),
            ]
        )
    tiles = count * heads
    for m, peer in ((m, peers(pairs)[m]) for m in chosen):
        for a, ref in enumerate((q_ref, k_ref, v_ref)):
            room = pieces[m].at[pl.ds(a * tiles, tiles)]
            copy = pltpu.make_async_copy(
                ref.at[pl.ds(first, count), pl.ds(peer * heads, heads)],
                room.reshape(count, heads, share, HEAD_DIM),
                sems.at[m, a],
            )
            copies += start_all([copy])
    if first == 0:
        wait_all(read)
        lane = lax.broadcasted_iota(jnp.int32, (SPAN, SPAN), 1)
        other = lax.broadcasted_iota(jnp.int32, (SPAN, SPAN), 0)
        half, within = lane // (pairs * share), lane % (pairs * share)
        source = (within // share * 2 + half) * share + within % share
        order = jnp.where(other == source, 1.0, 0.0).astype(jnp.bfloat16)
        places = jnp.dot(
            jnp.broadcast_to(plans[...].astype(jnp.bfloat16), (share, SPAN)),
            order,
            preferred_element_type=jnp.float32,
        )
        hit = other.astype(jnp.float32) == places[0:1]
        docs_here = jnp.dot(
            jnp.broadcast_to(docs[...].astype(jnp.bfloat16), (share, SPAN)),
            jnp.where(hit, 1.0, 0.0).astype(jnp.bfloat16),
            preferred_element_type=jnp.float32,
        )
        row = lax.broadcasted_iota(jnp.int32, (share, SPAN), 0)
        notes[0] = jnp.where(row == 0, places, docs_here).astype(jnp.bfloat16)
        copies += start_all(
            [
                pltpu.make_async_copy(notes, pieces[m].at[pl.ds(3 * tiles, 1)], note_sems.at[m])
                for m in chosen
            ]
        )
    wait_all(copies)


def pack(pairs, first, count, chosen, plan, docs, q, k, v):
    heads, share = q.shape[1] // pairs, q.shape[2]
    tiles = 3 * count * heads + (first == 0)
    shape = jax.ShapeDtypeStruct((tiles, share, HEAD_DIM), q.dtype)
    return pl.pallas_call(
        functools.partial(pack_kernel, pairs, heads, first, count, chosen),
        out_shape=[shape] * len(chosen),
        in_specs=[HBM] * 5,
        out_specs=[ANY] * len(chosen),
        scratch_shapes=[
            pltpu.VMEM((1, SPAN), jnp.int32),
            pltpu.VMEM((1, SPAN), jnp.int32),
            pltpu.VMEM((1, share, SPAN), q.dtype),
            pltpu.SemaphoreType.DMA((pairs, 3)),
            pltpu.SemaphoreType.DMA((pairs + 2,)),
        ],
        compiler_params=ROOM,
        name="pack",
    )(plan, docs, q, k, v)


def mark_kernel(x_ref, out_ref):
    pass


def mark(x):
    return pl.pallas_call(
        mark_kernel,
        out_shape=jax.ShapeDtypeStruct((8, SPAN), jnp.float32),
        in_specs=[ANY],
        out_specs=ANY,
        compiler_params=ROOM,
        name="mark",
    )(x)


def collect_kernel(pairs, share, start, marked, *rest):
    rest = rest[marked:]
    pieces = rest[:pairs]
    out_ref, sems = rest[pairs:]
    copies = [
        pltpu.make_async_copy(
            pieces[m].at[pl.ds(start, out_ref.shape[0])],
            out_ref.at[:, rows_of(peer, share), :],
            sems.at[m],
        )
        for m, peer in enumerate(peers(pairs))
    ]
    wait_all(start_all(copies))


def collect(pairs, start, stop, pieces, marked):
    _, share, width = pieces[0].shape
    return pl.pallas_call(
        functools.partial(collect_kernel, pairs, share, start, len(marked)),
        out_shape=jax.ShapeDtypeStruct((stop - start, pairs * share, width), pieces[0].dtype),
        in_specs=[ANY] * (pairs + len(marked)),
        out_specs=ANY,
        scratch_shapes=[pltpu.SemaphoreType.DMA((pairs,))],
        compiler_params=ROOM,
        name="collect",
    )(*marked, *pieces)


def attend_kernel(pairs, share, width, first, count, last, gain_ref, *rest):
    rest = list(rest)
    take = lambda k: [rest.pop(0) for _ in range(k)]
    given = take(3) if first else None
    queries, own, other = take(3)
    outs = take(pairs)
    kept = [] if last else take(3)
    state, mixed_rows, sems = rest
    half = pairs * share
    mine, side = place()
    heads = width // HEAD_DIM
    tiles = count * heads
    lower = side == 0
    if first:
        carry_doc = given[0][...]
        state[...] = given[1][...]
        lower_notes, upper_notes = given[2][:half], given[2][half:]
    else:
        carry_doc = jnp.full((1, SPAN), -1.0, jnp.float32)
        state[...] = jnp.zeros_like(state)
        lower_notes = jnp.where(lower, own[2 * tiles], other[2 * tiles])
        upper_notes = jnp.where(lower, other[2 * tiles], own[2 * tiles])
    if not last:
        kept[2][:half] = lower_notes
        kept[2][half:] = upper_notes
    gains = [gain_ref[pl.ds(mine * heads + h, 1), :] for h in range(heads)]

    def block(d, carry_doc):
        at = (first + d) // 2 * share
        said = (upper_notes if (first + d) % 2 else lower_notes)[at : at + share]
        said = said.astype(jnp.float32)
        said = jnp.where(lower, said, pltpu.roll(said, SPAN // 2, axis=1))
        place_s, doc_s = said[0:1], said[1:2]
        key_s = doc_s * SPAN + place_s
        key_t = jnp.transpose(jnp.broadcast_to(key_s, (SPAN, SPAN)))[:half]
        doc_t = jnp.floor(key_t * (1.0 / SPAN))
        allowed = jnp.logical_and(key_s <= key_t, key_s >= doc_t * SPAN)
        last_doc = jnp.broadcast_to(jnp.max(doc_s, axis=1, keepdims=True), (1, SPAN))
        match = doc_t == carry_doc
        tail = jnp.where(doc_s == last_doc, 1.0, 0.0).astype(jnp.bfloat16)
        keep = carry_doc == last_doc
        for h in range(heads):
            cols = slice(h * HEAD_DIM, (h + 1) * HEAD_DIM)
            tile = d * heads + h
            q = queries[tile]
            k, v = (
                jnp.concatenate([own[a * tiles + tile], other[a * tiles + tile]])
                for a in range(2)
            )
            turned = jnp.transpose(k)
            carry = state[h]
            scores = jnp.dot(q, turned, preferred_element_type=jnp.float32)
            carried = jnp.dot(q, carry.astype(jnp.bfloat16), preferred_element_type=jnp.float32)
            weights = jnp.where(allowed, scores, 0.0).astype(jnp.bfloat16)
            inner = jnp.dot(weights, v, preferred_element_type=jnp.float32)
            fresh = jnp.dot(turned * tail, v, preferred_element_type=jnp.float32)
            state[h] = fresh + jnp.where(keep, carry, 0.0)
            mixed = inner + jnp.where(match, carried, 0.0)
            scale = lax.rsqrt(jnp.mean(mixed * mixed, axis=-1, keepdims=True) + 1e-06)
            mixed_rows[d, :, cols] = (mixed * scale * gains[h]).astype(jnp.bfloat16)
        return last_doc

    copies = []
    for d in range(count):
        carry_doc = block(d, carry_doc)
        if d + 1 in (count // 2, count):
            done = pl.ds(0, count // 2) if d + 1 < count else pl.ds(count // 2, count - count // 2)
            copies += start_all(
                [
                    pltpu.make_async_copy(
                        mixed_rows.at[done, rows_of(peer, share), :],
                        outs[m].at[done],
                        sems.at[int(d + 1 == count), m],
                    )
                    for m, peer in enumerate(peers(pairs))
                ]
            )
    if not last:
        kept[0][...] = carry_doc
        kept[1][...] = state[...]
    wait_all(copies)


def attend(pairs, share, width, first, count, last, gain, queries, own, other, given):
    half, dtype = pairs * share, own.dtype
    state = (width // HEAD_DIM, HEAD_DIM, HEAD_DIM)
    kept = [
        jax.ShapeDtypeStruct((1, SPAN), jnp.float32),
        jax.ShapeDtypeStruct(state, jnp.float32),
        jax.ShapeDtypeStruct((2 * half, SPAN), dtype),
    ]
    kept, given = [] if last else kept, list(given) if first else []
    near = [
        pltpu.with_memory_space_constraint(x, pltpu.VMEM)
        for x in given + [queries, own, other]
    ]
    results = pl.pallas_call(
        functools.partial(attend_kernel, pairs, share, width, first, count, last),
        out_shape=[jax.ShapeDtypeStruct((count, share, width), dtype)] * pairs + kept,
        in_specs=[VMEM] * (4 + len(given)),
        out_specs=[ANY] * pairs + [VMEM] * len(kept),
        scratch_shapes=[
            pltpu.VMEM(state, jnp.float32),
            pltpu.VMEM((count, half, width), dtype),
            pltpu.SemaphoreType.DMA((2, pairs)),
        ],
        compiler_params=ROOM,
        name="attend",
    )(gain, *near)
    return results[:pairs], results[pairs:]


def unpack_kernel(pairs, width, spans, before, *rest):
    pieces = rest[before:]
    out_ref, sems = rest[-2:]
    copies = []
    for c, (first, count) in enumerate(spans):
        for m, peer in enumerate(peers(pairs)):
            come = pl.ds(pl.multiple_of(peer * width, width), width)
            copies.append(
                pltpu.make_async_copy(
                    pieces[c * pairs + m],
                    out_ref.at[pl.ds(first, count), :, come],
                    sems.at[c, m],
                )
            )
    wait_all(start_all(copies))


def unpack(n, width, spans, pieces, made):
    share, dtype = pieces[0].shape[1], pieces[0].dtype
    pairs = n // 2
    return pl.pallas_call(
        functools.partial(unpack_kernel, pairs, width, spans, len(made)),
        out_shape=jax.ShapeDtypeStruct((n, share, pairs * width), dtype),
        in_specs=[HBM] * len(made) + [ANY] * (pairs * len(spans)),
        out_specs=HBM,
        scratch_shapes=[pltpu.SemaphoreType.DMA((len(spans), pairs))],
        input_output_aliases={0: 0} if made else {},
        compiler_params=ROOM,
        name="unpack",
    )(*made, *pieces)


def swap(x, n, zero, one):
    return lax.ppermute(x, AXIS, [(i, i ^ (one if i & 1 else zero)) for i in range(n)])


def exchange(n, pieces):
    arrived = []
    for (zero, one), x in zip(slots(n // 2), pieces):
        arrived.append(swap(x, n, 2 * zero, 2 * one) if zero else x)
    return arrived


def heads_apart(n, q_store, k_store, v_store, plan, doc_ids, gain):
    share, pairs, full = SPAN // n, n // 2, q_store.shape[1]
    width = full // pairs
    stays = lambda a, *shape: pltpu.with_memory_space_constraint(a.reshape(shape), pltpu.HBM)
    heads = full // HEAD_DIM
    tiled = lambda a: a.reshape(n, share, heads, HEAD_DIM).transpose(0, 2, 1, 3)
    q, k, v = (stays(tiled(a), n, heads, share, HEAD_DIM) for a in (q_store, k_store, v_store))
    plan, docs = stays(plan, 1, SPAN), stays(doc_ids, 1, SPAN)
    gain = gain.reshape(heads, HEAD_DIM)
    parts = [c * n // sum(CHUNKS) for c in CHUNKS]
    spans = [(sum(parts[:c]), count) for c, count in enumerate(parts)]
    arrived = []
    for first, count in spans:
        order = [pairs // 2, *(k for k in range(pairs) if k != pairs // 2)]
        cut = pairs if first else 2
        packed = pack(pairs, first, count, order[:cut], plan, docs, q, k, v)
        if cut < pairs:
            packed += pack(pairs, first, count, order[cut:], plan, docs, q, k, v)
        pieces = [x for _, x in sorted(zip(order, packed), key=lambda pair: pair[0])]
        arrived.append(exchange(n, pieces))
    back, given, marked = [], None, []
    for (first, count), pieces in zip(spans, arrived):
        last = first + count == n
        marks = marked
        if not last:
            marks = marks + [mark(plan)]
        tiles = count * heads // pairs
        own = collect(pairs, tiles, pieces[0].shape[0], pieces, marks)
        other = swap(own, n, 1, 1)
        queries = collect(pairs, 0, tiles, pieces, [])
        pieces, given = attend(
            pairs, share, width, first, count, last, gain, queries, own, other, given
        )
        if not last:
            marked = [mark(pieces[-1])]
        back += exchange(n, pieces)
    made, cut = [], len(spans) - 1
    if cut:
        made = [unpack(n, width, spans[:cut], back[: cut * pairs], made)]
    return unpack(n, width, spans[cut:], back[cut * pairs :], made).reshape(SPAN, full)


def solution(mesh):
    n = mesh.shape[AXIS]

    def on_device(q_store, k_store, v_store, plan, doc_ids, gain):
        heads = q_store.shape[1] // HEAD_DIM
        paired = n & (n - 1) == 0
        tiled = q_store.shape[0] == SPAN and SPAN % n == 0 and (SPAN // n) % 8 == 0
        if paired and tiled and n >= 8 and heads % n == 0:
            return heads_apart(n, q_store, k_store, v_store, plan, doc_ids, gain)
        return at_home(q_store, k_store, v_store, plan, doc_ids, gain)

    return jax.shard_map(
        on_device,
        mesh=mesh,
        in_specs=(
            P(("groups", "context"), None),
            P(("groups", "context"), None),
            P(("groups", "context"), None),
            P(("groups", "context"), None),
            P(("groups", "context")),
            P(),
        ),
        out_specs=P(("groups", "context"), None),
        check_vma=False,
    )
```

```python
import functools

import jax
import jax.numpy as jnp
from jax import lax
from jax.experimental import pallas as pl
from jax.experimental.pallas import tpu as pltpu
from jax.sharding import PartitionSpec as P


HEAD_DIM = 128
SPAN = 128
AXIS = "context"


def entering(part, axis, combine, identity):
    place = lax.axis_index(axis)
    gathered = jax.tree.map(lambda a: lax.all_gather(a, axis), part)
    state = jax.tree.map(lambda a, e: jnp.zeros_like(a) + jnp.asarray(e, a.dtype), part, identity)

    def one(lap, state):
        return combine(
            state, jax.tree.map(lambda a: lax.dynamic_index_in_dim(a, lap, 0, False), gathered)
        )

    return lax.fori_loop(0, place, one, state)


def merge_states(earlier, later):
    early_state, early_doc = earlier
    late_state, late_doc = later
    keep_early = jnp.logical_or(early_doc == late_doc, late_doc < 0)
    merged = late_state + jnp.where(
        keep_early[:, None, None], early_state, jnp.zeros_like(early_state)
    )
    return (merged, jnp.where(late_doc < 0, early_doc, late_doc))


def at_home(q_store, k_store, v_store, plan, doc_ids, gain):
    token_count = q_store.shape[0]
    head_count = q_store.shape[1] // HEAD_DIM
    span_count = token_count // SPAN
    placed = plan.reshape(-1)
    inverse = (
        jnp.zeros((token_count,), jnp.int32)
        .at[placed]
        .set(jnp.arange(token_count, dtype=jnp.int32))
    )

    def settle(arrived):
        return jnp.take(arrived, inverse, axis=0).reshape(span_count, SPAN, head_count, HEAD_DIM)

    docs = doc_ids.reshape(span_count, SPAN)
    last_doc = docs[:, -1]
    query_rows, key_rows, value_rows = (
        lax.all_to_all(q_store, AXIS, split_axis=0, concat_axis=0, tiled=True),
        lax.all_to_all(k_store, AXIS, split_axis=0, concat_axis=0, tiled=True),
        lax.all_to_all(v_store, AXIS, split_axis=0, concat_axis=0, tiled=True),
    )
    keys_home = settle(key_rows)
    values_home = settle(value_rows)
    tail_mask = (docs == last_doc[:, None]).astype(jnp.bfloat16)
    span_states = jnp.einsum(
        "cshd,cshe->chde",
        keys_home * tail_mask[:, :, None, None],
        values_home,
        preferred_element_type=jnp.float32,
    )
    device_part = (span_states[0], last_doc)
    identity = (jnp.zeros_like(span_states[0]), jnp.full((1,), -1, jnp.int32))
    running = entering(device_part, AXIS, merge_states, identity)
    carry_states = running[0].astype(jnp.bfloat16)[None]
    queries = settle(query_rows)
    causal = jnp.arange(SPAN)[:, None] >= jnp.arange(SPAN)[None, :]
    allowed = jnp.logical_and(causal[None], docs[:, :, None] == docs[:, None, :])
    scores = jnp.einsum("cthd,cshd->chts", queries, keys_home, preferred_element_type=jnp.float32)
    weights = jnp.where(allowed[:, None], scores, 0.0).astype(jnp.bfloat16)
    inner = jnp.einsum("chts,cshe->cthe", weights, values_home, preferred_element_type=jnp.float32)
    match = (docs == running[1][:, None]).astype(jnp.bfloat16)
    carried = jnp.einsum(
        "cthd,chde->cthe",
        queries * match[:, :, None, None],
        carry_states,
        preferred_element_type=jnp.float32,
    )
    mixed = inner + carried
    scale = lax.rsqrt(jnp.mean(mixed * mixed, axis=-1, keepdims=True) + 1e-06)
    normed = (mixed * scale * gain.reshape(head_count, HEAD_DIM)).astype(jnp.bfloat16)
    normed = normed.reshape(token_count, head_count * HEAD_DIM)
    leaving = jnp.take(normed, placed, axis=0)
    return lax.all_to_all(leaving, AXIS, split_axis=0, concat_axis=0, tiled=True)


VMEM = pl.BlockSpec(memory_space=pltpu.VMEM)
ANY = pl.BlockSpec(memory_space=pl.ANY)
HBM = pl.BlockSpec(memory_space=pltpu.HBM)
ROOM = pltpu.CompilerParams(vmem_limit_bytes=24 << 20)
CHUNKS = (10, 6)


def slots(pairs):
    half, most = pairs // 2, 3 * pairs // 4
    far = [*range(most - 1, half - 1, -1), *range(pairs - 1, most - 1, -1)]
    near = [1, *range(pairs // 2 - 1, 1, -1)]
    return list(zip(far + near, near + sorted(far, reverse=True))) + [(0, 0)]


def early_slot(pairs):
    return min(pairs // 2 + 1, pairs - 2)


def place():
    me = lax.axis_index(AXIS)
    mine, side = lax.shift_right_logical(me, 1), jnp.bitwise_and(me, 1)
    return mine, side


def peers(pairs):
    mine, side = place()
    return [
        jnp.bitwise_xor(mine, jnp.where(side == 0, zero, one)) for zero, one in slots(pairs)
    ]


def start_all(copies):
    for copy in copies:
        copy.start()
    return copies


def wait_all(copies):
    for copy in copies:
        copy.wait()


def rows_of(pair, share):
    return pl.ds(pl.multiple_of(pair * share, share), share)


def pack_kernel(pairs, heads, first, count, chosen, plan_ref, doc_ref, q_ref, k_ref, v_ref, *rest):
    pieces = dict(zip(chosen, rest))
    plans, docs, notes, sems, note_sems = rest[len(chosen) :]
    share = SPAN // (2 * pairs)
    copies = []
    if first == 0:
        read = start_all(
            [
                pltpu.make_async_copy(plan_ref, plans, note_sems.at[pairs]),
                pltpu.make_async_copy(doc_ref, docs, note_sems.at[pairs + 1]),
            ]
        )
    tiles = count * heads
    for m, peer in ((m, peers(pairs)[m]) for m in chosen):
        for a, ref in enumerate((q_ref, k_ref, v_ref)):
            room = pieces[m].at[pl.ds(a * tiles, tiles)]
            copy = pltpu.make_async_copy(
                ref.at[pl.ds(first, count), pl.ds(peer * heads, heads)],
                room.reshape(count, heads, share, HEAD_DIM),
                sems.at[m, a],
            )
            copies += start_all([copy])
    if first == 0:
        wait_all(read)
        lane = lax.broadcasted_iota(jnp.int32, (SPAN, SPAN), 1)
        other = lax.broadcasted_iota(jnp.int32, (SPAN, SPAN), 0)
        half, within = lane // (pairs * share), lane % (pairs * share)
        source = (within // share * 2 + half) * share + within % share
        order = jnp.where(other == source, 1.0, 0.0).astype(jnp.bfloat16)
        places = jnp.dot(
            jnp.broadcast_to(plans[...].astype(jnp.bfloat16), (share, SPAN)),
            order,
            preferred_element_type=jnp.float32,
        )
        hit = other.astype(jnp.float32) == places[0:1]
        docs_here = jnp.dot(
            jnp.broadcast_to(docs[...].astype(jnp.bfloat16), (share, SPAN)),
            jnp.where(hit, 1.0, 0.0).astype(jnp.bfloat16),
            preferred_element_type=jnp.float32,
        )
        row = lax.broadcasted_iota(jnp.int32, (share, SPAN), 0)
        notes[0] = jnp.where(row == 0, places, docs_here).astype(jnp.bfloat16)
        copies += start_all(
            [
                pltpu.make_async_copy(notes, pieces[m].at[pl.ds(3 * tiles, 1)], note_sems.at[m])
                for m in chosen
            ]
        )
    wait_all(copies)


def pack(pairs, first, count, chosen, plan, docs, q, k, v):
    heads, share = q.shape[1] // pairs, q.shape[2]
    tiles = 3 * count * heads + (first == 0)
    shape = jax.ShapeDtypeStruct((tiles, share, HEAD_DIM), q.dtype)
    return pl.pallas_call(
        functools.partial(pack_kernel, pairs, heads, first, count, chosen),
        out_shape=[shape] * len(chosen),
        in_specs=[HBM] * 5,
        out_specs=[ANY] * len(chosen),
        scratch_shapes=[
            pltpu.VMEM((1, SPAN), jnp.int32),
            pltpu.VMEM((1, SPAN), jnp.int32),
            pltpu.VMEM((1, share, SPAN), q.dtype),
            pltpu.SemaphoreType.DMA((pairs, 3)),
            pltpu.SemaphoreType.DMA((pairs + 2,)),
        ],
        compiler_params=ROOM,
        name="pack",
    )(plan, docs, q, k, v)


def mark_kernel(x_ref, out_ref):
    pass


def mark(x):
    return pl.pallas_call(
        mark_kernel,
        out_shape=jax.ShapeDtypeStruct((8, SPAN), jnp.float32),
        in_specs=[ANY],
        out_specs=ANY,
        compiler_params=ROOM,
        name="mark",
    )(x)


def collect_kernel(pairs, share, start, marked, *rest):
    rest = rest[marked:]
    pieces = rest[:pairs]
    out_ref, sems = rest[pairs:]
    copies = [
        pltpu.make_async_copy(
            pieces[m].at[pl.ds(start, out_ref.shape[0])],
            out_ref.at[:, rows_of(peer, share), :],
            sems.at[m],
        )
        for m, peer in enumerate(peers(pairs))
    ]
    wait_all(start_all(copies))


def collect(pairs, start, stop, pieces, marked):
    _, share, width = pieces[0].shape
    return pl.pallas_call(
        functools.partial(collect_kernel, pairs, share, start, len(marked)),
        out_shape=jax.ShapeDtypeStruct((stop - start, pairs * share, width), pieces[0].dtype),
        in_specs=[ANY] * (pairs + len(marked)),
        out_specs=ANY,
        scratch_shapes=[pltpu.SemaphoreType.DMA((pairs,))],
        compiler_params=ROOM,
        name="collect",
    )(*marked, *pieces)


def attend_kernel(pairs, share, width, first, count, last, gain_ref, *rest):
    rest = list(rest)
    take = lambda k: [rest.pop(0) for _ in range(k)]
    given = take(3) if first else None
    queries, own, other = take(3)
    outs = take(pairs)
    kept = [] if last else take(3)
    state, mixed_rows, sems = rest
    half = pairs * share
    mine, side = place()
    heads = width // HEAD_DIM
    tiles = count * heads
    lower = side == 0
    if first:
        carry_doc = given[0][...]
        state[...] = given[1][...]
        lower_notes, upper_notes = given[2][:half], given[2][half:]
    else:
        carry_doc = jnp.full((1, SPAN), -1.0, jnp.float32)
        state[...] = jnp.zeros_like(state)
        lower_notes = jnp.where(lower, own[2 * tiles], other[2 * tiles])
        upper_notes = jnp.where(lower, other[2 * tiles], own[2 * tiles])
    if not last:
        kept[2][:half] = lower_notes
        kept[2][half:] = upper_notes
    gains = [gain_ref[pl.ds(mine * heads + h, 1), :] for h in range(heads)]

    def block(d, carry_doc):
        at = (first + d) // 2 * share
        said = (upper_notes if (first + d) % 2 else lower_notes)[at : at + share]
        said = said.astype(jnp.float32)
        said = jnp.where(lower, said, pltpu.roll(said, SPAN // 2, axis=1))
        place_s, doc_s = said[0:1], said[1:2]
        key_s = doc_s * SPAN + place_s
        key_t = jnp.transpose(jnp.broadcast_to(key_s, (SPAN, SPAN)))[:half]
        doc_t = jnp.floor(key_t * (1.0 / SPAN))
        allowed = jnp.logical_and(key_s <= key_t, key_s >= doc_t * SPAN)
        last_doc = jnp.broadcast_to(jnp.max(doc_s, axis=1, keepdims=True), (1, SPAN))
        match = doc_t == carry_doc
        tail = jnp.where(doc_s == last_doc, 1.0, 0.0).astype(jnp.bfloat16)
        keep = carry_doc == last_doc
        for h in range(heads):
            cols = slice(h * HEAD_DIM, (h + 1) * HEAD_DIM)
            tile = d * heads + h
            q = queries[tile]
            k, v = (
                jnp.concatenate([own[a * tiles + tile], other[a * tiles + tile]])
                for a in range(2)
            )
            turned = jnp.transpose(k)
            carry = state[h]
            scores = jnp.dot(q, turned, preferred_element_type=jnp.float32)
            carried = jnp.dot(q, carry.astype(jnp.bfloat16), preferred_element_type=jnp.float32)
            weights = jnp.where(allowed, scores, 0.0).astype(jnp.bfloat16)
            inner = jnp.dot(weights, v, preferred_element_type=jnp.float32)
            fresh = jnp.dot(turned * tail, v, preferred_element_type=jnp.float32)
            state[h] = fresh + jnp.where(keep, carry, 0.0)
            mixed = inner + jnp.where(match, carried, 0.0)
            scale = lax.rsqrt(jnp.mean(mixed * mixed, axis=-1, keepdims=True) + 1e-06)
            mixed_rows[d, :, cols] = (mixed * scale * gains[h]).astype(jnp.bfloat16)
        return last_doc

    copies = []
    for d in range(count):
        carry_doc = block(d, carry_doc)
        if d + 1 in (count // 2, count):
            done = pl.ds(0, count // 2) if d + 1 < count else pl.ds(count // 2, count - count // 2)
            copies += start_all(
                [
                    pltpu.make_async_copy(
                        mixed_rows.at[done, rows_of(peer, share), :],
                        outs[m].at[done],
                        sems.at[int(d + 1 == count), m],
                    )
                    for m, peer in enumerate(peers(pairs))
                ]
            )
    if not last:
        kept[0][...] = carry_doc
        kept[1][...] = state[...]
    wait_all(copies)


def attend(pairs, share, width, first, count, last, gain, queries, own, other, given):
    half, dtype = pairs * share, own.dtype
    state = (width // HEAD_DIM, HEAD_DIM, HEAD_DIM)
    kept = [
        jax.ShapeDtypeStruct((1, SPAN), jnp.float32),
        jax.ShapeDtypeStruct(state, jnp.float32),
        jax.ShapeDtypeStruct((2 * half, SPAN), dtype),
    ]
    kept, given = [] if last else kept, list(given) if first else []
    near = [
        pltpu.with_memory_space_constraint(x, pltpu.VMEM)
        for x in given + [queries, own, other]
    ]
    results = pl.pallas_call(
        functools.partial(attend_kernel, pairs, share, width, first, count, last),
        out_shape=[jax.ShapeDtypeStruct((count, share, width), dtype)] * pairs + kept,
        in_specs=[VMEM] * (4 + len(given)),
        out_specs=[ANY] * pairs + [VMEM] * len(kept),
        scratch_shapes=[
            pltpu.VMEM(state, jnp.float32),
            pltpu.VMEM((count, half, width), dtype),
            pltpu.SemaphoreType.DMA((2, pairs)),
        ],
        compiler_params=ROOM,
        name="attend",
    )(gain, *near)
    return results[:pairs], results[pairs:]


def unpack_kernel(pairs, width, spans, before, *rest):
    pieces = rest[before:]
    out_ref, sems = rest[-2:]
    copies = []
    for c, (first, count) in enumerate(spans):
        for m, peer in enumerate(peers(pairs)):
            come = pl.ds(pl.multiple_of(peer * width, width), width)
            copies.append(
                pltpu.make_async_copy(
                    pieces[c * pairs + m],
                    out_ref.at[pl.ds(first, count), :, come],
                    sems.at[c, m],
                )
            )
    wait_all(start_all(copies))


def unpack(n, width, spans, pieces, made):
    share, dtype = pieces[0].shape[1], pieces[0].dtype
    pairs = n // 2
    return pl.pallas_call(
        functools.partial(unpack_kernel, pairs, width, spans, len(made)),
        out_shape=jax.ShapeDtypeStruct((n, share, pairs * width), dtype),
        in_specs=[HBM] * len(made) + [ANY] * (pairs * len(spans)),
        out_specs=HBM,
        scratch_shapes=[pltpu.SemaphoreType.DMA((len(spans), pairs))],
        input_output_aliases={0: 0} if made else {},
        compiler_params=ROOM,
        name="unpack",
    )(*made, *pieces)


def swap(x, n, zero, one):
    return lax.ppermute(x, AXIS, [(i, i ^ (one if i & 1 else zero)) for i in range(n)])


def exchange(n, pieces):
    arrived = []
    for (zero, one), x in zip(slots(n // 2), pieces):
        arrived.append(swap(x, n, 2 * zero, 2 * one) if zero else x)
    return arrived


def heads_apart(n, q_store, k_store, v_store, plan, doc_ids, gain):
    share, pairs, full = SPAN // n, n // 2, q_store.shape[1]
    width = full // pairs
    stays = lambda a, *shape: pltpu.with_memory_space_constraint(a.reshape(shape), pltpu.HBM)
    heads = full // HEAD_DIM
    tiled = lambda a: a.reshape(n, share, heads, HEAD_DIM).transpose(0, 2, 1, 3)
    q, k, v = (stays(tiled(a), n, heads, share, HEAD_DIM) for a in (q_store, k_store, v_store))
    plan, docs = stays(plan, 1, SPAN), stays(doc_ids, 1, SPAN)
    gain = gain.reshape(heads, HEAD_DIM)
    parts = [c * n // sum(CHUNKS) for c in CHUNKS]
    spans = [(sum(parts[:c]), count) for c, count in enumerate(parts)]
    arrived = []
    for first, count in spans:
        order = sorted(range(pairs), key=lambda k: (k != early_slot(pairs), k))
        cut = pairs if first else 2
        packed = pack(pairs, first, count, order[:cut], plan, docs, q, k, v)
        if cut < pairs:
            packed += pack(pairs, first, count, order[cut:], plan, docs, q, k, v)
        pieces = [x for _, x in sorted(zip(order, packed), key=lambda pair: pair[0])]
        arrived.append(exchange(n, pieces))
    back, given, marked = [], None, []
    for (first, count), pieces in zip(spans, arrived):
        last = first + count == n
        marks = marked
        if not last:
            marks = marks + [mark(plan)]
        tiles = count * heads // pairs
        own = collect(pairs, tiles, pieces[0].shape[0], pieces, marks)
        other = swap(own, n, 1, 1)
        queries = collect(pairs, 0, tiles, pieces, [])
        pieces, given = attend(
            pairs, share, width, first, count, last, gain, queries, own, other, given
        )
        if not last:
            marked = [mark(pieces[-1])]
        back += exchange(n, pieces)
    made, cut = [], len(spans) - 1
    if cut:
        made = [unpack(n, width, spans[:cut], back[: cut * pairs], made)]
    return unpack(n, width, spans[cut:], back[cut * pairs :], made).reshape(SPAN, full)


def solution(mesh):
    n = mesh.shape[AXIS]

    def on_device(q_store, k_store, v_store, plan, doc_ids, gain):
        heads = q_store.shape[1] // HEAD_DIM
        paired = n & (n - 1) == 0
        tiled = q_store.shape[0] == SPAN and SPAN % n == 0 and (SPAN // n) % 8 == 0
        if paired and tiled and n >= 8 and heads % n == 0:
            return heads_apart(n, q_store, k_store, v_store, plan, doc_ids, gain)
        return at_home(q_store, k_store, v_store, plan, doc_ids, gain)

    return jax.shard_map(
        on_device,
        mesh=mesh,
        in_specs=(
            P(("groups", "context"), None),
            P(("groups", "context"), None),
            P(("groups", "context"), None),
            P(("groups", "context"), None),
            P(("groups", "context")),
            P(),
        ),
        out_specs=P(("groups", "context"), None),
        check_vma=False,
    )
```
